32 devices in a mesh: dp: 8 (over z, x), tensor: 4 (over y, core).
Axes of the slice: x: 2, y: 2, z: 4, core: 2. Of those that a mesh axis runs over, the one named last changes fastest.
Arguments:
- bag_items: bfloat16 [16384, 64, 128], P('dp', 'tensor'), may hold values from -1.1953125 to 1.1953125
- bag_lengths: int32 [2048, 64], P('dp', 'tensor'), may hold values from 0 to 16, as said below
- send_counts: int32 [8, 8], P('dp'), may hold values from 0 to 48, as said below
- cross_weight: bfloat16 [1, 8192, 8192], P(None, 'tensor', 'dp'), may hold values from -0.0625 to 0.0625
- cross_bias: float32 [1, 8192], P(None, 'tensor'), may hold values from -3 to 3
Outputs:
- crossed: bfloat16 [2048, 8192], P('dp', 'tensor')
The draws below stay inside these ranges and needn't reach their ends.
Inputs may be any that keep to these rules, and one draw needn't show every extreme that they name: `bag_lengths`: for every feature, the bags of the 256 rows of one aligned block hold 2048 items together; bags may be empty; in every aligned block and feature some bag holds exactly 16 items. `send_counts`: every row and every column sums to 256; each row has eight nonzero entries, one of them may be on the diagonal; no entry exceeds 48 and every row has an entry equal to 48.
All inputs are finite; a program needn't handle non-finite values.
Results may differ from the reference program's by a relative error of at most 0.0053.
Values may be sent and summed in bfloat16 or wider, within the bound.
No kernel may reach another device: no remote copies, remote signals or barrier semaphores. Data moves between devices by JAX's collectives and lax.ppermute only.
A program may use at most 128 MiB of HBM per device.

```python
import jax
import jax.numpy as jnp
from jax import lax

F = 64
E = 128
WIDE = 8192
ROWS_DEV = 256
BAG = 8
LAYERS = 1
SLOTS = 2048
CAP = 48
BATCH = 2048


def draw_bag_lengths(key, part):
    block_count = BATCH // ROWS_DEV
    half_rows = ROWS_DEV // 2
    key_delta, key_pick = jax.random.split(jax.random.fold_in(key, 5), 2)
    deltas = jax.random.randint(key_delta, (block_count, F, half_rows), -BAG, BAG + 1).astype(jnp.int32)
    picked = jax.random.randint(key_pick, (block_count, F), 0, half_rows).astype(jnp.int32)
    pair_index = lax_iota(block_count, half_rows)
    deltas = jnp.where(pair_index == picked[:, :, None], jnp.int32(BAG), deltas)
    lengths = jnp.stack([BAG + deltas, BAG - deltas], axis=-1).reshape(block_count, F, ROWS_DEV)
    return jnp.transpose(lengths, (0, 2, 1)).reshape(BATCH, F).astype(jnp.int32)


def lax_iota(block_count, half_rows):
    return jnp.broadcast_to(jnp.arange(half_rows, dtype=jnp.int32)[None, None, :], (block_count, F, half_rows))


def draw_send_counts(key, part):
    device_count = BATCH // ROWS_DEV
    key_outer, key_inner, key_shift, key_spread = jax.random.split(jax.random.fold_in(key, 17), 4)
    outer_perm = jax.random.permutation(key_outer, device_count).astype(jnp.int32)
    inner_perm = jax.random.permutation(key_inner, device_count).astype(jnp.int32)
    shift_list = jax.random.permutation(key_shift, device_count)[:8].astype(jnp.int32)
    remain = ROWS_DEV - CAP
    base_share = remain // 7
    extra_rows = remain - 7 * base_share
    share_list = [CAP] + [base_share + (1 if which < extra_rows else 0) for which in range(7)]
    spread_most = max(min(base_share - 1, CAP - base_share - 1), 0)
    deltas = jax.random.randint(key_spread, (3,), 0, spread_most + 1).astype(jnp.int32)
    nothing = jnp.zeros((), jnp.int32)
    perturb = jnp.stack([nothing, deltas[0], -deltas[0], deltas[1], -deltas[1], deltas[2], -deltas[2], nothing])
    share_array = jnp.array(share_list, jnp.int32) + perturb
    sources = jnp.arange(device_count, dtype=jnp.int32)
    counts = jnp.zeros((device_count, device_count), jnp.int32)
    for which_share in range(8):
        targets = outer_perm[(inner_perm + shift_list[which_share]) % device_count]
        counts = counts.at[sources, targets].add(share_array[which_share])
    return counts


def block_levels(stream_key, shape, cuts, smallest, top_value):
    def one(dim, blocks):
        heights = jax.random.uniform(jax.random.fold_in(jax.random.fold_in(stream_key, 6), dim), (blocks,), jnp.float32, smallest / len(cuts), top_value / len(cuts))
        return jnp.repeat(jnp.exp(heights), shape[dim] // blocks).reshape((-1,) + (1,) * (len(shape) - dim - 1))

    factor_of = one(*cuts[0])
    for cut in cuts[1:]:
        factor_of = factor_of * one(*cut)
    return factor_of


def scatter_about(key, shape, width, limit, cuts=(), kind=jnp.bfloat16):
    values = jax.random.normal(key, shape, jnp.float32) * width
    if len(cuts) > 0:
        values = block_levels(key, shape, cuts, -0.22, 0.18) * values
    return jnp.clip(values, min=-limit, max=limit).astype(kind)


def setup_inputs(seed: int = 0) -> dict:
    keys = jax.random.split(jax.random.key(seed), 6)
    return {
        "bag_items": scatter_about(keys[0], (BATCH * BAG, F, E), 0.2, 1.1953125, ((0, 8), (1, 4))),
        "bag_lengths": draw_bag_lengths(jax.random.fold_in(keys[5], 71), 0),
        "send_counts": draw_send_counts(jax.random.fold_in(keys[5], 71), 0),
        "cross_weight": scatter_about(keys[3], (LAYERS, WIDE, WIDE), WIDE ** -0.5, 0.0625, ((1, 4), (2, 8))),
        "cross_bias": scatter_about(keys[4], (LAYERS, WIDE), 0.5, 3.0, ((1, 4),), jnp.float32),
    }


def reference(bag_items, bag_lengths, send_counts, cross_weight, cross_bias):
    block_count = BATCH // ROWS_DEV
    lengths = bag_lengths.reshape(block_count, ROWS_DEV, F).astype(jnp.int32)
    bag_ends = jnp.cumsum(lengths, axis=1).astype(jnp.int32)
    positions = jnp.arange(SLOTS, dtype=jnp.int32)
    block_base = jnp.arange(block_count, dtype=jnp.int32)[:, None] * ROWS_DEV

    def locate(block_end):
        return jnp.searchsorted(block_end, positions, side="right").astype(jnp.int32)

    def pool_feature(feature):
        feature_ends = lax.dynamic_index_in_dim(bag_ends, feature, 2, keepdims=False)
        local_ids = jax.vmap(locate)(feature_ends).astype(jnp.int32)
        segment_ids = (local_ids + block_base).reshape(-1).astype(jnp.int32)
        items = lax.dynamic_index_in_dim(bag_items, feature, 1, keepdims=False).astype(jnp.float32)
        return jax.ops.segment_sum(items, segment_ids, num_segments=BATCH)

    pooled_all = lax.map(pool_feature, jnp.arange(F, dtype=jnp.int32))
    pooled = jnp.transpose(pooled_all, (1, 0, 2)).reshape(BATCH, F * E).astype(jnp.bfloat16)

    counts = send_counts.astype(jnp.int32)
    send_end = jnp.cumsum(counts, axis=1).astype(jnp.int32)
    send_start = send_end - counts
    recv_start = jnp.cumsum(counts, axis=0).astype(jnp.int32) - counts
    local_rows = jnp.arange(ROWS_DEV, dtype=jnp.int32)
    target_block = jnp.sum((send_end[:, None, :] <= local_rows[None, :, None]).astype(jnp.int32), axis=2).astype(jnp.int32)
    start_at = jnp.take_along_axis(send_start, target_block, axis=1)
    recv_at = jnp.take_along_axis(recv_start, target_block, axis=1)
    destination = (target_block * ROWS_DEV + recv_at + local_rows[None, :] - start_at).reshape(-1).astype(jnp.int32)
    cross_input = jnp.zeros_like(pooled).at[destination].set(pooled)

    base_rows = cross_input.astype(jnp.float32)
    state = cross_input
    for layer_index in range(LAYERS):
        product = jnp.dot(state, cross_weight[layer_index].T, preferred_element_type=jnp.float32)
        state = (base_rows * (product + cross_bias[layer_index]) + state.astype(jnp.float32)).astype(jnp.bfloat16)
    return state
```

```python
import functools

import jax
import jax.numpy as jnp
from jax import lax
from jax.experimental import pallas as pl
from jax.experimental.pallas import tpu as pltpu
from jax.sharding import Mesh
from jax.sharding import PartitionSpec as P

CAP = 48
BF16 = jnp.bfloat16
F32 = jnp.float32
I32 = jnp.int32
ANY = pl.ANY
VMEM = pltpu.VMEM
SMEM = pltpu.SMEM


def params(mib):
    return pltpu.CompilerParams(vmem_limit_bytes=mib << 20)


def pool_kernel(groups, share, quarter, count_ref, length_ref, items_ref, *rest):
    out_refs = rest[: len(groups)]
    items, wide, by_feat, first, last, pooled, sems = rest[len(groups) :]
    slots, feats, width = items.shape
    rows = length_ref.shape[1]
    step = slots // sems.shape[0]
    copies = []
    for k in range(sems.shape[0]):
        part = pl.ds(k * step, step)
        copy = pltpu.make_async_copy(items_ref.at[part], items.at[part], sems.at[k])
        copy.start()
        copies.append(copy)

    row_id = lax.broadcasted_iota(I32, (rows, rows), 0)
    col_id = lax.broadcasted_iota(I32, (rows, rows), 1)
    lower = jnp.where(col_id <= row_id, 1.0, 0.0).astype(BF16)
    strict = jnp.where(col_id < row_id, 1.0, 0.0).astype(BF16)
    lengths = length_ref[...].astype(F32).astype(BF16)
    dims = (((1,), (1,)), ((), ()))
    ends = lax.dot_general(lower, lengths, dims, preferred_element_type=F32).astype(I32)
    starts = lax.dot_general(strict, lengths, dims, preferred_element_type=F32).astype(I32)
    for f in range(feats):
        first[f] = jnp.broadcast_to(starts[:, f : f + 1], (rows, width))
        last[f] = jnp.broadcast_to(ends[:, f : f + 1], (rows, width))

    for k in range(sems.shape[0]):
        copies[k].wait()
        part = pl.ds(k * step, step)
        wide[...] = items[part].astype(F32).reshape(step * feats, width)
        for f in range(feats):
            by_feat[f, part, :] = wide[pl.ds(f, step, stride=feats), :].astype(BF16)

    lane = lax.broadcasted_iota(I32, (rows, width), 1)

    @pl.loop(0, feats)
    def _(f):
        low = first[f]
        high = last[f]
        total = jnp.zeros((rows, width), F32)
        for k in range(slots // (2 * width)):
            tiles = []
            for half in range(2):
                where = lane + (2 * k + half) * width
                inside = (where >= low) & (where < high)
                tiles.append(jnp.where(inside, 1.0, 0.0).astype(BF16))
            total += jnp.dot(
                jnp.concatenate(tiles, axis=1),
                by_feat[f, pl.ds(2 * k * width, 2 * width), :],
                preferred_element_type=F32,
            )
        pooled[:, pl.ds(pl.multiple_of(f * width, width), width)] = total.astype(BF16)

    slot = lax.broadcasted_iota(I32, (CAP, rows), 0)
    source = lax.broadcasted_iota(I32, (CAP, rows), 1)
    begin = []
    at = jnp.int32(0)
    for p in range(count_ref.shape[1]):
        begin.append(at)
        at = at + count_ref[0, p]
    for g, group in enumerate(groups):
        picks = []
        for b in range(share):
            for a in group:
                p = a * share + b
                hit = (source == slot + begin[p]) & (slot < count_ref[0, p])
                picks.append(jnp.where(hit, 1.0, 0.0).astype(BF16))
        pick = jnp.concatenate(picks, axis=0)
        for q in range(out_refs[g].shape[0]):
            moved = jnp.dot(
                pick, pooled[:, q * quarter : (q + 1) * quarter], preferred_element_type=F32
            )
            out_refs[g][q] = moved.astype(BF16)


def pool(bag_items, bag_lengths, send_counts, groups, share, quarters):
    slots, feats, width = bag_items.shape
    rows = bag_lengths.shape[0]
    quarter = feats * width // quarters
    chunks = 8
    return pl.pallas_call(
        functools.partial(pool_kernel, groups, share, quarter),
        out_shape=[
            jax.ShapeDtypeStruct((quarters, share * len(g) * CAP, quarter), BF16) for g in groups
        ],
        in_specs=[
            pl.BlockSpec(memory_space=SMEM),
            pl.BlockSpec(memory_space=VMEM),
            pl.BlockSpec(memory_space=ANY),
        ],
        out_specs=[pl.BlockSpec(memory_space=VMEM) for _ in groups],
        scratch_shapes=[
            VMEM((slots, feats, width), BF16),
            VMEM((slots // chunks * feats, width), F32),
            VMEM((feats, slots, width), BF16),
            VMEM((feats, rows, width), I32),
            VMEM((feats, rows, width), I32),
            VMEM((rows, feats * width), BF16),
            pltpu.SemaphoreType.DMA((chunks,)),
        ],
        compiler_params=params(48),
        cost_estimate=pl.CostEstimate(
            flops=2 * rows * slots * feats * width,
            bytes_accessed=2 * slots * feats * width,
            transcendentals=0,
        ),
        name="pool",
    )(send_counts, bag_lengths.T, bag_items)


def order_kernel(group, share, rows, place_ref, counts_ref, slots_ref, out_ref):
    sources = slots_ref.shape[0]
    lane = lax.broadcasted_iota(I32, (rows, sources * CAP), 1)
    place = lax.broadcasted_iota(I32, (rows, sources * CAP), 0)
    b = place_ref[0]
    for g, a in enumerate(group):
        want = jnp.full((rows, sources * CAP), -1, I32)
        at = jnp.int32(0)
        for k in range(sources):
            count = counts_ref[k, a * share + b]
            slot = lane - k * CAP
            want = jnp.where((slot >= 0) & (slot < count), slot + at, want)
            at = at + count
        pick = jnp.where(want == place, 1.0, 0.0).astype(BF16)
        got = slots_ref[:, g * CAP : (g + 1) * CAP, :].reshape(sources * CAP, slots_ref.shape[2])
        out_ref[g] = jnp.dot(pick, got, preferred_element_type=F32).astype(BF16)


def order(place, counts, slots, group, share, rows):
    quarter = slots.shape[2]
    return pl.pallas_call(
        functools.partial(order_kernel, group, share, rows),
        out_shape=jax.ShapeDtypeStruct((len(group), rows, quarter), BF16),
        in_specs=[
            pl.BlockSpec(memory_space=SMEM),
            pl.BlockSpec(memory_space=SMEM),
            pl.BlockSpec(memory_space=VMEM),
        ],
        out_specs=pl.BlockSpec(memory_space=VMEM),
        compiler_params=params(32),
        cost_estimate=pl.CostEstimate(
            flops=2 * len(group) * rows * slots.shape[0] * CAP * quarter,
            bytes_accessed=2 * slots.size,
            transcendentals=0,
        ),
        name="order",
    )(place, counts, slots)


def multiply_kernel(count, spot_ref, *refs):
    pieces = refs[:count]
    own_ref, other_ref, out_ref, held = refs[count:]

    @pl.when(pl.program_id(0) == 0)
    def _():
        for j in range(count):
            held[spot_ref[j]] = pieces[j][...].reshape(held.shape[1:])

    quarter = held.shape[2]
    half = count // 2
    total = None
    for j in range(count):
        weight = own_ref if j < half else other_ref
        part = lax.dot_general(
            held[j],
            weight[:, (j % half) * quarter : (j % half + 1) * quarter],
            (((1,), (1,)), ((), ())),
            preferred_element_type=F32,
        )
        total = part if total is None else total + part
    out_ref[...] = total.astype(BF16).reshape(out_ref.shape)


def multiply(spots, pieces, own, other, offset, tile):
    blocks, rows, quarter = pieces[0].shape
    count = len(pieces)
    outs, depth = other.shape
    base = offset // tile
    return pl.pallas_call(
        functools.partial(multiply_kernel, count),
        out_shape=jax.ShapeDtypeStruct((blocks, rows, outs), BF16),
        grid=(outs // tile,),
        in_specs=[pl.BlockSpec(memory_space=SMEM)]
        + [
            pl.BlockSpec((blocks, rows, quarter), lambda n: (0, 0, 0), pipeline_mode=pl.Buffered(1))
            for _ in pieces
        ]
        + [
            pl.BlockSpec((tile, depth), lambda n: (n + base, 0)),
            pl.BlockSpec((tile, depth), lambda n: (n, 0)),
        ],
        out_specs=pl.BlockSpec((blocks, rows, tile), lambda n: (0, 0, n)),
        scratch_shapes=[VMEM((count, blocks * rows, quarter), BF16)],
        compiler_params=params(32),
        cost_estimate=pl.CostEstimate(
            flops=4 * blocks * rows * outs * depth,
            bytes_accessed=2 * (2 * outs * depth + blocks * rows * (outs + count * quarter)),
            transcendentals=0,
        ),
        name="multiply",
    )(spots, *pieces, own, other)


def pick(index, options):
    value = options[0][1]
    for which, other in options[1:]:
        value = jnp.where(index == which, other, value)
    return value


def shards(bag_items, bag_lengths, send_counts, cross_weight, cross_bias):
    line, share = lax.axis_size("a"), lax.axis_size("b")
    tall = lax.axis_size("y")
    quarters = tall * 2
    rows = bag_lengths.shape[0]
    a, b = lax.axis_index("a"), lax.axis_index("b")
    y, c = lax.axis_index("y"), lax.axis_index("c")
    swap = [(0, 1), (1, 0)]
    edge = line // 4
    groups = [
        list(range(edge)) + list(range(line - edge, line)),
        list(range(edge, line - edge)),
    ]

    weight = cross_weight[0]
    outs = weight.shape[0]
    parts = 2
    each = outs // parts
    others = [
        lax.ppermute(weight[n * each : (n + 1) * each], "b", swap) for n in range(parts)
    ]
    counts = lax.all_gather(send_counts, ("a", "b"), axis=0, tiled=True)
    padded = pool(bag_items, bag_lengths, send_counts, groups, share, quarters)

    place = b.reshape(1).astype(I32)
    ordered, pieces = [], []
    for g, group in enumerate(groups):
        mixed = lax.all_to_all(padded[g], ("y", "c"), 0, 0, tiled=True)
        mixed = mixed.reshape(line * share, len(group) * CAP, mixed.shape[2])
        slots = lax.all_to_all(mixed, ("a", "b"), 0, 0, tiled=True)
        mine = order(place, counts, slots, group, share, rows)
        ordered.append(mine)
        if tall == 2:
            far = lax.ppermute(mine, "y", swap)
            near = [(y, mine), (1 - y, far)]
        else:
            every = lax.all_gather(mine, "y", axis=0)
            near = [(jnp.int32(k), every[k]) for k in range(tall)]
        found = [(k, c, piece) for k, piece in near]
        found += [(k, 1 - c, lax.ppermute(piece, "c", swap)) for k, piece in near]
        pieces.append(found)

    half = quarters // 2
    spots = []
    for k, core, _ in pieces[0]:
        quarter_id = k * 2 + core
        spots.append(jnp.where(quarter_id // half == b, 0, half) + quarter_id % half)
    spots = jnp.stack(spots).astype(I32)

    tile = min(512, each)
    columns = []
    for n in range(parts):
        block = {}
        for g, group in enumerate(groups):
            partial = multiply(
                spots, [piece for _, _, piece in pieces[g]], weight, others[n], n * each, tile
            )
            for k, which in enumerate(group):
                block[which] = partial[k]
        up = down = None
        for s in range(1, line):
            send_up = pick(a, [(i, block[line - s + i]) for i in range(s)])
            send_down = pick(a, [(line - 1 - i, block[s - 1 - i]) for i in range(s)])
            if up is not None:
                send_up = send_up + up
                send_down = send_down + down
            up = lax.ppermute(send_up, "a", [(i, i + 1) for i in range(s)])
            down = lax.ppermute(
                send_down, "a", [(line - 1 - i, line - 2 - i) for i in range(s)]
            )
        mine = pick(a, [(i, block[i]) for i in range(line)])
        columns.append(mine.astype(F32) + up.astype(F32) + down.astype(F32))
    product = jnp.concatenate(columns, axis=1)

    blocks = [None] * line
    for g, group in enumerate(groups):
        for k, which in enumerate(group):
            blocks[which] = ordered[g][k]
    back = lax.all_to_all(jnp.stack(blocks), "a", 0, 0, tiled=True)
    back = lax.all_to_all(back, ("y", "c"), 0, 0, tiled=True)
    base = jnp.transpose(back, (1, 0, 2)).reshape(rows, -1).astype(F32)
    return (base * (product + cross_bias[0]) + base).astype(BF16)


def solution(mesh):
    owners, tensor = mesh.devices.shape
    split = Mesh(
        mesh.devices.reshape(tensor, owners // tensor, tensor // 2, 2), ("a", "b", "y", "c")
    )
    dp, tp = ("a", "b"), ("y", "c")
    return jax.shard_map(
        shards,
        mesh=split,
        in_specs=(
            P(dp, tp, None),
            P(dp, tp),
            P(dp, None),
            P(None, tp, dp),
            P(None, tp),
        ),
        out_specs=P(dp, tp),
        check_vma=False,
    )
```

```python
import functools

import jax
import jax.numpy as jnp
from jax import lax
from jax.experimental import pallas as pl
from jax.experimental.pallas import tpu as pltpu
from jax.sharding import Mesh
from jax.sharding import PartitionSpec as P

CAP = 48
HEAD = 16
BF16 = jnp.bfloat16
F32 = jnp.float32
I32 = jnp.int32
ANY = pl.ANY
VMEM = pltpu.VMEM
SMEM = pltpu.SMEM
SMALL = pl.CostEstimate(flops=1, bytes_accessed=1, transcendentals=0)


def params(mib):
    return pltpu.CompilerParams(vmem_limit_bytes=mib << 20)


def pool_kernel(groups, share, quarter, count_ref, spot_ref, length_ref, items_ref, *rest):
    out_refs = rest[: len(groups)]
    items, wide, by_feat, first, last, pooled, sems = rest[len(groups) :]
    slots, feats, width = items.shape
    rows = length_ref.shape[1]
    step = slots // sems.shape[0]
    copies = []
    for k in range(sems.shape[0]):
        part = pl.ds(k * step, step)
        copy = pltpu.make_async_copy(items_ref.at[part], items.at[part], sems.at[k])
        copy.start()
        copies.append(copy)

    row_id = lax.broadcasted_iota(I32, (rows, rows), 0)
    col_id = lax.broadcasted_iota(I32, (rows, rows), 1)
    lower = jnp.where(col_id <= row_id, 1.0, 0.0).astype(BF16)
    strict = jnp.where(col_id < row_id, 1.0, 0.0).astype(BF16)
    lengths = length_ref[...].astype(F32).astype(BF16)
    dims = (((1,), (1,)), ((), ()))
    ends = lax.dot_general(lower, lengths, dims, preferred_element_type=F32).astype(I32)
    starts = lax.dot_general(strict, lengths, dims, preferred_element_type=F32).astype(I32)
    for f in range(feats):
        first[f] = jnp.broadcast_to(starts[:, f : f + 1], (rows, width))
        last[f] = jnp.broadcast_to(ends[:, f : f + 1], (rows, width))

    for k in range(sems.shape[0]):
        copies[k].wait()
        part = pl.ds(k * step, step)
        wide[...] = items[part].astype(F32).reshape(step * feats, width)
        for f in range(feats):
            by_feat[f, part, :] = wide[pl.ds(f, step, stride=feats), :].astype(BF16)

    lane = lax.broadcasted_iota(I32, (rows, width), 1)

    @pl.loop(0, feats, unroll=2)
    def _(f):
        low = first[f]
        high = last[f]
        total = jnp.zeros((rows, width), F32)
        for k in range(slots // (2 * width)):
            tiles = []
            for half in range(2):
                where = lane + (2 * k + half) * width
                inside = (where >= low) & (where < high)
                tiles.append(jnp.where(inside, 1.0, 0.0).astype(BF16))
            total += jnp.dot(
                jnp.concatenate(tiles, axis=1),
                by_feat[f, pl.ds(2 * k * width, 2 * width), :],
                preferred_element_type=F32,
            )
        pooled[:, pl.ds(pl.multiple_of(f * width, width), width)] = total.astype(BF16)

    slot = lax.broadcasted_iota(I32, (CAP, rows), 0)
    source = lax.broadcasted_iota(I32, (CAP, rows), 1)
    begin = []
    at = jnp.int32(0)
    for p in range(count_ref.shape[1]):
        begin.append(at)
        at = at + count_ref[0, p]
    for g, group in enumerate(groups):
        picks = []
        for b in range(share):
            for a in group:
                p = a * share + b
                hit = (source == slot + begin[p]) & (slot < count_ref[0, p])
                picks.append(jnp.where(hit, 1.0, 0.0).astype(BF16))
        pick = jnp.concatenate(picks, axis=0)
        body = len(group) * CAP
        for q in range(out_refs[g].shape[0]):
            at = pl.multiple_of(spot_ref[g, q] * quarter, quarter)
            moved = jnp.dot(
                pick, pooled[:, pl.ds(at, quarter)], preferred_element_type=F32
            ).astype(BF16)
            for b in range(share):
                out_refs[g][q, b, :body] = moved[b * body : (b + 1) * body]
        if g > 0:
            continue
        which = lax.broadcasted_iota(I32, (HEAD, quarter), 0)
        for b in range(share):
            head = jnp.zeros((HEAD, quarter), F32)
            for p in range(b, count_ref.shape[1], share):
                head = jnp.where(which == p // share, count_ref[0, p].astype(F32), head)
            for q in range(out_refs[g].shape[0]):
                out_refs[g][q, b, body:] = head.astype(BF16)


def pool(bag_items, bag_lengths, send_counts, spots, groups, share, quarters):
    slots, feats, width = bag_items.shape
    rows = bag_lengths.shape[0]
    quarter = feats * width // quarters
    chunks = 8
    return pl.pallas_call(
        functools.partial(pool_kernel, groups, share, quarter),
        out_shape=[
            jax.ShapeDtypeStruct(
                (quarters, share, len(g) * CAP + (0 if k else HEAD), quarter), BF16
            )
            for k, g in enumerate(groups)
        ],
        in_specs=[
            pl.BlockSpec(memory_space=SMEM),
            pl.BlockSpec(memory_space=SMEM),
            pl.BlockSpec(memory_space=VMEM),
            pl.BlockSpec(memory_space=ANY),
        ],
        out_specs=[pl.BlockSpec(memory_space=VMEM) for _ in groups],
        scratch_shapes=[
            VMEM((slots, feats, width), BF16),
            VMEM((slots // chunks * feats, width), F32),
            VMEM((feats, slots, width), BF16),
            VMEM((feats, rows, width), I32),
            VMEM((feats, rows, width), I32),
            VMEM((rows, feats * width), BF16),
            pltpu.SemaphoreType.DMA((chunks,)),
        ],
        compiler_params=params(48),
        cost_estimate=SMALL,
        name="pool",
    )(send_counts, spots, bag_lengths.T, bag_items)


def order_kernel(group, rows, slots_ref, head_ref, out_ref):
    sources = slots_ref.shape[0]
    width = sources * CAP
    lane = lax.broadcasted_iota(I32, (1, width), 1).astype(F32)
    place = lax.broadcasted_iota(I32, (rows, width), 0).astype(F32)
    for g, a in enumerate(group):
        want = jnp.full((1, width), -1.0, F32)
        at = jnp.zeros((1, width), F32)
        for k in range(sources):
            count = head_ref[k, a : a + 1, :].astype(F32)
            count = jnp.concatenate([count] * (width // count.shape[1]), axis=1)
            slot = lane - k * CAP
            want = jnp.where((slot >= 0) & (slot < count), slot + at, want)
            at = at + count
        pick = jnp.where(want == place, 1.0, 0.0).astype(BF16)
        got = slots_ref[:, g * CAP : (g + 1) * CAP, :].reshape(width, slots_ref.shape[2])
        out_ref[g] = jnp.dot(pick, got, preferred_element_type=F32).astype(BF16)


def order(slots, head, group, rows):
    quarter = slots.shape[2]
    return pl.pallas_call(
        functools.partial(order_kernel, group, rows),
        out_shape=jax.ShapeDtypeStruct((len(group), rows, quarter), BF16),
        in_specs=[pl.BlockSpec(memory_space=VMEM), pl.BlockSpec(memory_space=VMEM)],
        out_specs=pl.BlockSpec(memory_space=VMEM),
        compiler_params=params(32),
        cost_estimate=SMALL,
        name="order",
    )(slots, head)


def multiply_kernel(count, cuts, spot_ref, *refs):
    pieces = refs[:count]
    own_ref = refs[count]
    other_refs = refs[count + 1 : count + 1 + len(cuts)]
    out_ref, held = refs[count + 1 + len(cuts) :]
    step = pl.program_id(0)

    @pl.when(step == 0)
    def _():
        for j in range(count):
            held[spot_ref[j]] = pieces[j][...].reshape(held.shape[1:])

    quarter = held.shape[2]
    half = count // 2

    def run(other_ref):
        total = None
        for j in range(count):
            weight = own_ref if j < half else other_ref
            part = lax.dot_general(
                held[j],
                weight[:, (j % half) * quarter : (j % half + 1) * quarter],
                (((1,), (1,)), ((), ())),
                preferred_element_type=F32,
            )
            total = part if total is None else total + part
        out_ref[...] = total.astype(BF16).reshape(out_ref.shape)

    for (low, high), other_ref in zip(cuts, other_refs):
        pl.when((step >= low) & (step < high))(functools.partial(run, other_ref))


def multiply(spots, pieces, own, others, offset, tile):
    blocks, rows, quarter = pieces[0].shape
    count = len(pieces)
    depth = own.shape[1]
    base = offset // tile
    cuts, at = [], 0
    for other in others:
        cuts.append((at, at + other.shape[0] // tile))
        at = cuts[-1][1]

    def other_spec(low, high):
        return pl.BlockSpec((tile, depth), lambda n: (jnp.clip(n - low, 0, high - low - 1), 0))

    return pl.pallas_call(
        functools.partial(multiply_kernel, count, cuts),
        out_shape=jax.ShapeDtypeStruct((blocks, rows, at * tile), BF16),
        grid=(at,),
        in_specs=[pl.BlockSpec(memory_space=SMEM)]
        + [
            pl.BlockSpec((blocks, rows, quarter), lambda n: (0, 0, 0), pipeline_mode=pl.Buffered(1))
            for _ in pieces
        ]
        + [pl.BlockSpec((tile, depth), lambda n: (n + base, 0))]
        + [other_spec(*cut) for cut in cuts],
        out_specs=pl.BlockSpec((blocks, rows, tile), lambda n: (0, 0, n)),
        scratch_shapes=[VMEM((count, blocks * rows, quarter), BF16)],
        compiler_params=params(32),
        cost_estimate=SMALL,
        name="multiply",
    )(spots, *pieces, own, *others)


def pick(index, options):
    value = options[0][1]
    for which, other in options[1:]:
        value = jnp.where(index == which, other, value)
    return value


def shards(bag_items, bag_lengths, send_counts, cross_weight, cross_bias):
    line, share = lax.axis_size("a"), lax.axis_size("b")
    tall = lax.axis_size("y")
    quarters = tall * 2
    rows = bag_lengths.shape[0]
    a, b = lax.axis_index("a"), lax.axis_index("b")
    y, c = lax.axis_index("y"), lax.axis_index("c")
    swap = [(0, 1), (1, 0)]
    edge = line // 4
    groups = [
        list(range(edge)) + list(range(line - edge, line)),
        list(range(edge, line - edge)),
    ]

    weight = cross_weight[0]
    outs = weight.shape[0]
    eighth = outs // 8
    cuts = [(0, 3 * eighth), (3 * eighth, 5 * eighth), (5 * eighth, outs)]
    parts = [(0, 2), (2, 3)]

    def fetch(which, gate=None):
        piece = weight[cuts[which][0] : cuts[which][1]]
        if gate is not None:
            piece, _ = lax.optimization_barrier((piece, gate))
        return lax.ppermute(piece, "b", swap)

    plain = jnp.arange(quarters, dtype=I32)
    if tall == 2:
        near = jnp.stack([(y ^ (k // 2)) * 2 + (c ^ (k % 2)) for k in range(4)]).astype(I32)
    else:
        near = plain
    others = [fetch(0)]
    padded = pool(
        bag_items, bag_lengths, send_counts, jnp.stack([plain, near]), groups, share, quarters
    )

    def mix(sent, relative):
        if not relative:
            return lax.all_to_all(sent, ("y", "c"), 0, 0, tiled=True)
        far = lax.ppermute(sent[2:], "y", swap)
        side = lax.ppermute(sent[1], "c", swap)
        cross = lax.ppermute(far[1], "c", swap)
        got = [sent[0], side, far[0], cross]
        return jnp.stack(
            [pick(near[q], [(k, got[k]) for k in range(4)]) for q in range(4)]
        )

    mixed = [mix(padded[0], False)]
    mixed[0], others[0] = lax.optimization_barrier((mixed[0], others[0]))
    late, _ = lax.optimization_barrier((padded[1], mixed[0]))
    mixed.append(mix(late, tall == 2))
    others.append(fetch(1, mixed[0]))

    ordered, pieces = [], []
    head = None
    for g, group in enumerate(groups):
        sent = mixed[g].reshape(line * share, mixed[g].shape[2], mixed[g].shape[3])
        slots = lax.all_to_all(sent, ("a", "b"), 0, 0, tiled=True)
        if head is None:
            head = slots[:, len(group) * CAP :, : bag_items.shape[2]]
        mine = order(slots, head, group, rows)
        ordered.append(mine)
        if tall == 2:
            far = lax.ppermute(mine, "y", swap)
            found = [(y, mine), (1 - y, far)]
        else:
            every = lax.all_gather(mine, "y", axis=0)
            found = [(jnp.int32(k), every[k]) for k in range(tall)]
        if g == 0:
            others.append(fetch(2, found[-1][1]))
        found = [(k, c, piece) for k, piece in found] + [
            (k, 1 - c, lax.ppermute(piece, "c", swap)) for k, piece in found
        ]
        pieces.append(found)

    half = quarters // 2
    spots = []
    for k, core, _ in pieces[0]:
        quarter_id = k * 2 + core
        spots.append(jnp.where(quarter_id // half == b, 0, half) + quarter_id % half)
    spots = jnp.stack(spots).astype(I32)

    columns = []
    gate = None
    for first, last in parts:
        block = {}
        for g, group in enumerate(groups):
            taken = [piece for _, _, piece in pieces[g]]
            if gate is not None:
                taken, _ = lax.optimization_barrier((taken, gate))
            partial = multiply(spots, taken, weight, others[first:last], cuts[first][0], eighth)
            for k, which in enumerate(group):
                block[which] = partial[k]
        up = down = None
        for s in range(1, line):
            send_up = pick(a, [(i, block[line - s + i]) for i in range(s)])
            send_down = pick(a, [(line - 1 - i, block[s - 1 - i]) for i in range(s)])
            if up is not None:
                send_up = send_up + up
                send_down = send_down + down
            if s == 2:
                gate = send_up
            up = lax.ppermute(send_up, "a", [(i, i + 1) for i in range(s)])
            down = lax.ppermute(
                send_down, "a", [(line - 1 - i, line - 2 - i) for i in range(s)]
            )
        mine = pick(a, [(i, block[i]) for i in range(line)])
        columns.append(mine.astype(F32) + up.astype(F32) + down.astype(F32))
    product = jnp.concatenate(columns, axis=1)

    blocks = [None] * line
    for g, group in enumerate(groups):
        for k, which in enumerate(group):
            blocks[which] = ordered[g][k]
    back = lax.all_to_all(jnp.stack(blocks), "a", 0, 0, tiled=True)
    back = lax.all_to_all(back, ("y", "c"), 0, 0, tiled=True)
    base = jnp.transpose(back, (1, 0, 2)).reshape(rows, -1).astype(F32)
    return (base * (product + cross_bias[0]) + base).astype(BF16)


def solution(mesh):
    owners, tensor = mesh.devices.shape
    split = Mesh(
        mesh.devices.reshape(tensor, owners // tensor, tensor // 2, 2), ("a", "b", "y", "c")
    )
    dp, tp = ("a", "b"), ("y", "c")
    return jax.shard_map(
        shards,
        mesh=split,
        in_specs=(
            P(dp, tp, None),
            P(dp, tp),
            P(dp, None),
            P(None, tp, dp),
            P(None, tp),
        ),
        out_specs=P(dp, tp),
        check_vma=False,
    )
```

```python
import functools

import jax
import jax.numpy as jnp
from jax import lax
from jax.experimental import pallas as pl
from jax.experimental.pallas import tpu as pltpu
from jax.sharding import Mesh
from jax.sharding import PartitionSpec as P

CAP = 48
HEAD = 16
BF16 = jnp.bfloat16
F32 = jnp.float32
I32 = jnp.int32
ANY = pl.ANY
VMEM = pltpu.VMEM
SMEM = pltpu.SMEM
SMALL = pl.CostEstimate(flops=1, bytes_accessed=1, transcendentals=0)


def params(mib):
    return pltpu.CompilerParams(vmem_limit_bytes=mib << 20)


def pool_kernel(groups, share, quarter, whole, count_ref, spot_ref, length_ref, items_ref, *rest):
    out_refs = rest[: len(groups)]
    items, wide, by_feat, first, last, pooled, sems = rest[len(groups) :]
    slots, feats, width = items.shape
    rows = length_ref.shape[1]
    step = slots // sems.shape[0]
    copies = []
    for k in range(sems.shape[0]):
        part = pl.ds(k * step, step)
        if whole:
            source = items_ref.at[part]
        else:
            start = pl.multiple_of(spot_ref[spot_ref.shape[0] - 1] * feats, feats)
            source = items_ref.at[part, pl.ds(start, feats)]
        copy = pltpu.make_async_copy(source, items.at[part], sems.at[k])
        copy.start()
        copies.append(copy)

    row_id = lax.broadcasted_iota(I32, (rows, rows), 0)
    col_id = lax.broadcasted_iota(I32, (rows, rows), 1)
    lower = jnp.where(col_id <= row_id, 1.0, 0.0).astype(BF16)
    strict = jnp.where(col_id < row_id, 1.0, 0.0).astype(BF16)
    lengths = length_ref[...].astype(F32).astype(BF16)
    dims = (((1,), (1,)), ((), ()))
    ends = lax.dot_general(lower, lengths, dims, preferred_element_type=F32).astype(I32)
    starts = lax.dot_general(strict, lengths, dims, preferred_element_type=F32).astype(I32)
    for f in range(feats):
        first[f] = jnp.broadcast_to(starts[:, f : f + 1], (rows, width))
        last[f] = jnp.broadcast_to(ends[:, f : f + 1], (rows, width))

    for k in range(sems.shape[0]):
        copies[k].wait()
        part = pl.ds(k * step, step)
        wide[...] = items[part].astype(F32).reshape(step * feats, width)
        for f in range(feats):
            by_feat[f, part, :] = wide[pl.ds(f, step, stride=feats), :].astype(BF16)

    lane = lax.broadcasted_iota(I32, (rows, width), 1)

    @pl.loop(0, feats, unroll=2)
    def _(f):
        low = first[f]
        high = last[f]
        total = jnp.zeros((rows, width), F32)
        for k in range(slots // (2 * width)):
            tiles = []
            for half in range(2):
                where = lane + (2 * k + half) * width
                inside = (where >= low) & (where < high)
                tiles.append(jnp.where(inside, 1.0, 0.0).astype(BF16))
            total += jnp.dot(
                jnp.concatenate(tiles, axis=1),
                by_feat[f, pl.ds(2 * k * width, 2 * width), :],
                preferred_element_type=F32,
            )
        pooled[:, pl.ds(pl.multiple_of(f * width, width), width)] = total.astype(BF16)

    slot = lax.broadcasted_iota(I32, (CAP, rows), 0)
    source = lax.broadcasted_iota(I32, (CAP, rows), 1)
    begin = []
    at = jnp.int32(0)
    for p in range(count_ref.shape[1]):
        begin.append(at)
        at = at + count_ref[0, p]
    for g, group in enumerate(groups):
        picks = []
        for b in range(share):
            for a in group:
                p = a * share + b
                hit = (source == slot + begin[p]) & (slot < count_ref[0, p])
                picks.append(jnp.where(hit, 1.0, 0.0).astype(BF16))
        pick = jnp.concatenate(picks, axis=0)
        body = len(group) * CAP
        for q in range(out_refs[g].shape[0]):
            at = pl.multiple_of(spot_ref[q] * quarter, quarter)
            moved = jnp.dot(
                pick, pooled[:, pl.ds(at, quarter)], preferred_element_type=F32
            ).astype(BF16)
            for b in range(share):
                out_refs[g][q, b, :body] = moved[b * body : (b + 1) * body]
        if g > 0:
            continue
        which = lax.broadcasted_iota(I32, (HEAD, quarter), 0)
        for b in range(share):
            head = jnp.zeros((HEAD, quarter), F32)
            for p in range(b, count_ref.shape[1], share):
                head = jnp.where(which == p // share, count_ref[0, p].astype(F32), head)
            for q in range(out_refs[g].shape[0]):
                out_refs[g][q, b, body:] = head.astype(BF16)


def pool(bag_items, lengths, send_counts, spots, groups, share, quarter):
    slots, whole, width = bag_items.shape
    feats, rows = lengths.shape
    quarters = feats * width // quarter
    chunks = 8
    return pl.pallas_call(
        functools.partial(pool_kernel, groups, share, quarter, feats == whole),
        out_shape=[
            jax.ShapeDtypeStruct(
                (quarters, share, len(g) * CAP + (0 if k else HEAD), quarter), BF16
            )
            for k, g in enumerate(groups)
        ],
        in_specs=[
            pl.BlockSpec(memory_space=SMEM),
            pl.BlockSpec(memory_space=SMEM),
            pl.BlockSpec(memory_space=VMEM),
            pl.BlockSpec(memory_space=ANY),
        ],
        out_specs=[pl.BlockSpec(memory_space=VMEM) for _ in groups],
        scratch_shapes=[
            VMEM((slots, feats, width), BF16),
            VMEM((slots // chunks * feats, width), F32),
            VMEM((feats, slots, width), BF16),
            VMEM((feats, rows, width), I32),
            VMEM((feats, rows, width), I32),
            VMEM((rows, feats * width), BF16),
            pltpu.SemaphoreType.DMA((chunks,)),
        ],
        compiler_params=params(48),
        cost_estimate=SMALL,
        name="pool",
    )(send_counts, spots, lengths, bag_items)


def order_kernel(group, rows, slots_ref, head_ref, out_ref):
    sources = slots_ref.shape[0]
    width = sources * CAP
    lane = lax.broadcasted_iota(I32, (1, width), 1).astype(F32)
    place = lax.broadcasted_iota(I32, (rows, width), 0).astype(F32)
    for g, a in enumerate(group):
        want = jnp.full((1, width), -1.0, F32)
        at = jnp.zeros((1, width), F32)
        for k in range(sources):
            count = head_ref[k, a : a + 1, :].astype(F32)
            count = jnp.concatenate([count] * (width // count.shape[1]), axis=1)
            slot = lane - k * CAP
            want = jnp.where((slot >= 0) & (slot < count), slot + at, want)
            at = at + count
        pick = jnp.where(want == place, 1.0, 0.0).astype(BF16)
        got = slots_ref[:, g * CAP : (g + 1) * CAP, :].reshape(width, slots_ref.shape[2])
        out_ref[g] = jnp.dot(pick, got, preferred_element_type=F32).astype(BF16)


def order(slots, head, group, rows):
    quarter = slots.shape[2]
    return pl.pallas_call(
        functools.partial(order_kernel, group, rows),
        out_shape=jax.ShapeDtypeStruct((len(group), rows, quarter), BF16),
        in_specs=[pl.BlockSpec(memory_space=VMEM), pl.BlockSpec(memory_space=VMEM)],
        out_specs=pl.BlockSpec(memory_space=VMEM),
        compiler_params=params(32),
        cost_estimate=SMALL,
        name="order",
    )(slots, head)


def cut_kernel(source_ref, out_ref):
    out_ref[...] = source_ref[...]


def cut(weight, low, high, tile):
    depth = weight.shape[1]
    return pl.pallas_call(
        cut_kernel,
        out_shape=jax.ShapeDtypeStruct((high - low, depth), BF16),
        grid=((high - low) // tile,),
        in_specs=[pl.BlockSpec((tile, depth), lambda n: (n + low // tile, 0))],
        out_specs=pl.BlockSpec((tile, depth), lambda n: (n, 0)),
        compiler_params=params(60),
        cost_estimate=SMALL,
        name="cut",
    )(weight)


def multiply_kernel(counts, spans, spot_ref, place_ref, *refs):
    groups, count = counts
    pieces = refs[: groups * count]
    own_ref = refs[groups * count]
    other_refs = refs[groups * count + 1 : groups * count + 1 + len(spans)]
    out_refs = refs[groups * count + 1 + len(spans) : -1]
    held = refs[-1]
    rows = out_refs[0].shape[0]
    step = pl.program_id(0)

    @pl.when(step == 0)
    def _():
        for g in range(groups):
            for j in range(count):
                piece = pieces[g * count + j]
                for k in range(piece.shape[0]):
                    which = g * piece.shape[0] + k
                    at = pl.multiple_of(place_ref[which] * rows, rows)
                    held[spot_ref[j], pl.ds(at, rows), :] = piece[k]

    quarter = held.shape[2]
    half = count // 2

    def run(other_ref):
        total = None
        for j in range(count):
            weight = own_ref if j < half else other_ref
            part = lax.dot_general(
                held[j],
                weight[:, (j % half) * quarter : (j % half + 1) * quarter],
                (((1,), (1,)), ((), ())),
                preferred_element_type=F32,
            )
            total = part if total is None else total + part
        for k, out_ref in enumerate(out_refs):
            out_ref[...] = total[k * rows : (k + 1) * rows].astype(BF16)

    for (low, high), other_ref in zip(spans, other_refs):
        pl.when((step >= low) & (step < high))(functools.partial(run, other_ref))


def multiply(spots, places, groups, own, others, offset, tile):
    blocks, rows, quarter = groups[0][0].shape
    count = len(groups[0])
    depth = own.shape[1]
    base = offset // tile
    total = blocks * len(groups)
    spans, at = [], 0
    for other in others:
        spans.append((at, at + other.shape[0] // tile))
        at = spans[-1][1]

    def other_spec(low, high):
        return pl.BlockSpec((tile, depth), lambda n: (jnp.clip(n - low, 0, high - low - 1), 0))

    return pl.pallas_call(
        functools.partial(multiply_kernel, (len(groups), count), spans),
        out_shape=[jax.ShapeDtypeStruct((rows, at * tile), BF16) for _ in range(total)],
        grid=(at,),
        in_specs=[pl.BlockSpec(memory_space=SMEM)] * 2
        + [
            pl.BlockSpec((blocks, rows, quarter), lambda n: (0, 0, 0), pipeline_mode=pl.Buffered(1))
            for _ in range(count * len(groups))
        ]
        + [pl.BlockSpec((tile, depth), lambda n: (n + base, 0))]
        + [other_spec(*span) for span in spans],
        out_specs=[pl.BlockSpec((rows, tile), lambda n: (0, n)) for _ in range(total)],
        scratch_shapes=[VMEM((count, total * rows, quarter), BF16)],
        compiler_params=params(60),
        cost_estimate=SMALL,
        name="multiply",
    )(spots, places, *[piece for group in groups for piece in group], own, *others)


def finish_kernel(end_ref, own_end, own_mid, outer, near, far, base_ref, bias_ref, *rest):
    out_ref = rest[-1]
    base = base_ref[0].astype(F32)
    is_end = end_ref[0] == 1

    def run(sums):
        product = sums[0][...].astype(F32)
        for extra in sums[1:]:
            product += extra[...].astype(F32)
        out_ref[...] = (base * (product + bias_ref[...]) + base).astype(BF16)

    pl.when(is_end)(functools.partial(run, (own_end, outer)))
    pl.when(jnp.logical_not(is_end))(functools.partial(run, (own_mid, near, far)))


def finish(is_end, sums, base, bias, offset, tile, onto=None):
    quarters, rows, quarter = base.shape
    first = offset // tile
    per = quarter // tile
    more = [] if onto is None else [onto]
    return pl.pallas_call(
        finish_kernel,
        out_shape=jax.ShapeDtypeStruct((rows, quarters * quarter), BF16),
        grid=(sums[0].shape[1] // tile,),
        in_specs=[pl.BlockSpec(memory_space=SMEM)]
        + [pl.BlockSpec((rows, tile), lambda n: (0, n))] * 5
        + [
            pl.BlockSpec((1, rows, tile), lambda n: ((n + first) // per, 0, (n + first) % per)),
            pl.BlockSpec((1, tile), lambda n: (0, n + first)),
        ]
        + [pl.BlockSpec(memory_space=ANY) for _ in more],
        out_specs=pl.BlockSpec((rows, tile), lambda n: (0, n + first)),
        input_output_aliases={8: 0} if more else {},
        compiler_params=params(60),
        cost_estimate=SMALL,
        name="finish",
    )(is_end, *sums, base, bias, *more)


def pick(index, options):
    value = options[0][1]
    for which, other in options[1:]:
        value = jnp.where(index == which, other, value)
    return value


def shards(bag_items, bag_lengths, send_counts, cross_weight, cross_bias):
    line, share = lax.axis_size("a"), lax.axis_size("b")
    tall = lax.axis_size("y")
    quarters = tall * 2
    rows = bag_lengths.shape[0]
    a, b = lax.axis_index("a"), lax.axis_index("b")
    y, c = lax.axis_index("y"), lax.axis_index("c")
    swap = [(0, 1), (1, 0)]
    edge = line // 4
    groups = [
        list(range(edge, line - edge)),
        list(range(edge)) + list(range(line - edge, line)),
    ]

    weight = cross_weight[0]
    outs = weight.shape[0]
    eighth = outs // 8
    tile = 2 * eighth
    parts = [(0, tile), (tile, 2 * tile), (2 * tile, outs)]

    def fetch(which, source):
        return lax.ppermute(cut(source, *parts[which], tile), "b", swap)

    quarter = bag_items.shape[1] * bag_items.shape[2] // quarters
    lengths = bag_lengths.T
    others = [fetch(0, weight), fetch(1, weight)]
    mixed = []
    if tall == 2:
        feats = bag_items.shape[1] // 2
        near = [(y ^ (k // 2)) * 2 + (c ^ (k % 2)) for k in range(4)]

        def half_pool(side):
            spots = jnp.stack([c, 1 - c, side]).astype(I32)
            part = lax.dynamic_slice_in_dim(lengths, side * feats, feats, 0)
            return list(pool(bag_items, part, send_counts, spots, groups, share, quarter))

        leaving = half_pool(1 - y)
        away = [lax.ppermute(piece, "y", swap) for piece in leaving]
        staying = half_pool(y)
        for g in range(2):
            staying[g], others[g] = lax.optimization_barrier((staying[g], others[g]))
            side = lax.ppermute(staying[g][1], "c", swap)
            cross = lax.ppermute(away[g][1], "c", swap)
            got = [staying[g][0], side, away[g][0], cross]
            mixed.append(
                jnp.stack([pick(near[q], [(k, got[k]) for k in range(4)]) for q in range(4)])
            )
    else:
        spots = jnp.arange(quarters, dtype=I32)
        for padded in pool(bag_items, lengths, send_counts, spots, groups, share, quarter):
            mixed.append(lax.all_to_all(padded, ("y", "c"), 0, 0, tiled=True))

    upper = a >= 2
    is_end = ((a == 0) | (a == 3)).astype(I32).reshape(1)
    flip = jnp.where(upper, 0, 1).astype(I32)
    places = jnp.stack([flip, 1 - flip])
    inward, middle, outward = [(0, 1), (3, 2)], [(1, 2), (2, 1)], [(1, 0), (2, 3)]

    ordered, pieces = [], []
    head = None
    for g, group in enumerate(groups):
        sent = mixed[g].reshape(line * share, mixed[g].shape[2], mixed[g].shape[3])
        slots = lax.all_to_all(sent, ("a", "b"), 0, 0, tiled=True)
        if head is None:
            head = slots[:, len(group) * CAP :, : bag_items.shape[2]]
        if g == 1 and line == 4:
            far1, near1 = multiply(spots, places, [pieces[0]], weight, others[:2], 0, tile)
            in2 = lax.ppermute(far1, "a", inward)
            in3 = lax.ppermute(near1, "a", inward)
            slots, far1 = lax.optimization_barrier((slots, far1))
        mine = order(slots, head, group, rows)
        if g == 0:
            late, mine = lax.optimization_barrier((weight, mine))
            others.append(fetch(2, late))
        ordered.append(mine)
        if tall == 2:
            far = lax.ppermute(mine, "y", swap)
            found = [(y, mine), (1 - y, far)]
        else:
            every = lax.all_gather(mine, "y", axis=0)
            found = [(jnp.int32(k), every[k]) for k in range(tall)]
        found = [(k, c, piece) for k, piece in found] + [
            (k, 1 - c, lax.ppermute(piece, "c", swap)) for k, piece in found
        ]
        pieces.append([piece for _, _, piece in found])
        spots = [k * 2 + core for k, core, _ in found]
        half = quarters // 2
        spots = jnp.stack([jnp.where(q // half == b, 0, half) + q % half for q in spots])
        spots = spots.astype(I32)

    blocks = [None] * line
    for g, group in enumerate(groups):
        for k, which in enumerate(group):
            blocks[which] = ordered[g][k]
    middle_piece = len(pieces[1]) // 2
    stacked, pieces[1][middle_piece] = lax.optimization_barrier(
        (jnp.stack(blocks), pieces[1][middle_piece])
    )
    back = lax.all_to_all(stacked, "a", 0, 0, tiled=True)

    if line != 4:
        where = jnp.arange(line, dtype=I32)
        columns = []
        for held, low in ((others[:2], 0), (others[2:], parts[2][0])):
            block = {}
            for g, group in enumerate(groups):
                partial = multiply(spots, where, [pieces[g]], weight, held, low, tile)
                block.update(zip(group, partial))
            up = down = None
            for s in range(1, line):
                send_up = pick(a, [(i, block[line - s + i]) for i in range(s)])
                send_down = pick(a, [(line - 1 - i, block[s - 1 - i]) for i in range(s)])
                if up is not None:
                    send_up = send_up + up
                    send_down = send_down + down
                up = lax.ppermute(send_up, "a", [(i, i + 1) for i in range(s)])
                down = lax.ppermute(
                    send_down, "a", [(line - 1 - i, line - 2 - i) for i in range(s)]
                )
            mine = pick(a, [(i, block[i]) for i in range(line)])
            columns.append(mine.astype(F32) + up.astype(F32) + down.astype(F32))
        back = lax.all_to_all(back, ("y", "c"), 0, 0, tiled=True)
        base = jnp.transpose(back, (1, 0, 2)).reshape(rows, -1).astype(F32)
        return (base * (jnp.concatenate(columns, axis=1) + cross_bias[0]) + base).astype(BF16)

    far0, near0 = multiply(spots, places, [pieces[1]], weight, others[:2], 0, tile)
    in1 = lax.ppermute(far0, "a", inward)
    both, far0 = lax.optimization_barrier((pieces, far0))
    mid3 = lax.ppermute(far1 + in2, "a", middle)
    mid2 = lax.ppermute(far0 + in1, "a", middle)
    out3 = lax.ppermute(near0 + mid2, "a", outward)
    sums = (near0, near1, out3, in3, mid3)
    back = lax.all_to_all(back, ("y", "c"), 0, 0, tiled=True)

    far1, near1, far0, near0 = multiply(
        spots, jnp.concatenate([places, places + 2]), both, weight, others[2:], parts[2][0], tile
    )
    result = finish(is_end, sums, back, cross_bias, 0, tile)
    in1 = lax.ppermute(far0, "a", inward)
    in2 = lax.ppermute(far1, "a", inward)
    mid2 = lax.ppermute(far0 + in1, "a", middle)
    in3 = lax.ppermute(near1, "a", inward)
    mid3 = lax.ppermute(far1 + in2, "a", middle)
    out3 = lax.ppermute(near0 + mid2, "a", outward)
    sums = (near0, near1, out3, in3, mid3)
    return finish(is_end, sums, back, cross_bias, parts[2][0], tile, result)


def solution(mesh):
    owners, tensor = mesh.devices.shape
    split = Mesh(
        mesh.devices.reshape(tensor, owners // tensor, tensor // 2, 2), ("a", "b", "y", "c")
    )
    dp, tp = ("a", "b"), ("y", "c")
    return jax.shard_map(
        shards,
        mesh=split,
        in_specs=(
            P(dp, tp, None),
            P(dp, tp),
            P(dp, None),
            P(None, tp, dp),
            P(None, tp),
        ),
        out_specs=P(dp, tp),
        check_vma=False,
    )
```

```python
import functools

import jax
import jax.numpy as jnp
from jax import lax
from jax.experimental import pallas as pl
from jax.experimental.pallas import tpu as pltpu
from jax.sharding import Mesh
from jax.sharding import PartitionSpec as P

CAP = 48
HEAD = 16
BF16 = jnp.bfloat16
F32 = jnp.float32
I32 = jnp.int32
ANY = pl.ANY
VMEM = pltpu.VMEM
SMEM = pltpu.SMEM
SMALL = pl.CostEstimate(flops=1, bytes_accessed=1, transcendentals=0)


def params(mib):
    return pltpu.CompilerParams(vmem_limit_bytes=mib << 20)


def pool_kernel(groups, share, quarter, whole, count_ref, spot_ref, length_ref, items_ref, *rest):
    out_refs = rest[: len(groups)]
    items, wide, by_feat, last, pooled, sems = rest[len(groups) :]
    slots, feats, width = items.shape
    rows = length_ref.shape[1]
    step = slots // sems.shape[0]
    copies = []
    for k in range(sems.shape[0]):
        part = pl.ds(k * step, step)
        if whole:
            source = items_ref.at[part]
        else:
            start = pl.multiple_of(spot_ref[spot_ref.shape[0] - 1] * feats, feats)
            source = items_ref.at[part, pl.ds(start, feats)]
        copy = pltpu.make_async_copy(source, items.at[part], sems.at[k])
        copy.start()
        copies.append(copy)

    row_id = lax.broadcasted_iota(I32, (rows, rows), 0)
    col_id = lax.broadcasted_iota(I32, (rows, rows), 1)
    lower = jnp.where(col_id <= row_id, 1.0, 0.0).astype(BF16)
    lengths = length_ref[...].astype(F32).astype(BF16)
    dims = (((1,), (1,)), ((), ()))
    ends = lax.dot_general(lower, lengths, dims, preferred_element_type=F32).astype(I32)
    for f in range(feats):
        last[f] = jnp.broadcast_to(ends[:, f : f + 1], (rows, width))

    for k in range(sems.shape[0]):
        copies[k].wait()
        part = pl.ds(k * step, step)
        wide[...] = items[part].astype(F32).reshape(step * feats, width)
        for f in range(feats):
            by_feat[f, part, :] = wide[pl.ds(f, step, stride=feats), :].astype(BF16)

    lane = lax.broadcasted_iota(I32, (1, width), 1)
    top = lax.broadcasted_iota(I32, (rows, width), 0) == 0

    @pl.loop(0, feats, unroll=2)
    def _(f):
        high = last[f]
        tiles = []
        for k in range(slots // width):
            tiles.append(jnp.where(lane + k * width < high, 1.0, 0.0).astype(BF16))
        total = jnp.dot(jnp.concatenate(tiles, axis=1), by_feat[f], preferred_element_type=F32)
        above = jnp.where(top, 0.0, pltpu.roll(total, 1, 0))
        pooled[:, pl.ds(pl.multiple_of(f * width, width), width)] = (total - above).astype(BF16)

    slot = lax.broadcasted_iota(I32, (CAP, rows), 0)
    source = lax.broadcasted_iota(I32, (CAP, rows), 1)
    begin = []
    at = jnp.int32(0)
    for p in range(count_ref.shape[1]):
        begin.append(at)
        at = at + count_ref[0, p]
    for g, group in enumerate(groups):
        picks = []
        for b in range(share):
            for a in group:
                p = a * share + b
                hit = (source == slot + begin[p]) & (slot < count_ref[0, p])
                picks.append(jnp.where(hit, 1.0, 0.0).astype(BF16))
        pick = jnp.concatenate(picks, axis=0)
        body = len(group) * CAP
        for q in range(out_refs[g].shape[0]):
            at = pl.multiple_of(spot_ref[q] * quarter, quarter)
            moved = jnp.dot(
                pick, pooled[:, pl.ds(at, quarter)], preferred_element_type=F32
            ).astype(BF16)
            for b in range(share):
                out_refs[g][q, b, :body] = moved[b * body : (b + 1) * body]
        if g > 0:
            continue
        which = lax.broadcasted_iota(I32, (HEAD, quarter), 0)
        for b in range(share):
            head = jnp.zeros((HEAD, quarter), F32)
            for p in range(b, count_ref.shape[1], share):
                head = jnp.where(which == p // share, count_ref[0, p].astype(F32), head)
            for q in range(out_refs[g].shape[0]):
                out_refs[g][q, b, body:] = head.astype(BF16)


def pool(bag_items, lengths, send_counts, spots, groups, share, quarter):
    slots, whole, width = bag_items.shape
    feats, rows = lengths.shape
    quarters = feats * width // quarter
    chunks = 8
    return pl.pallas_call(
        functools.partial(pool_kernel, groups, share, quarter, feats == whole),
        out_shape=[
            jax.ShapeDtypeStruct(
                (quarters, share, len(g) * CAP + (0 if k else HEAD), quarter), BF16
            )
            for k, g in enumerate(groups)
        ],
        in_specs=[
            pl.BlockSpec(memory_space=SMEM),
            pl.BlockSpec(memory_space=SMEM),
            pl.BlockSpec(memory_space=VMEM),
            pl.BlockSpec(memory_space=ANY),
        ],
        out_specs=[pl.BlockSpec(memory_space=VMEM) for _ in groups],
        scratch_shapes=[
            VMEM((slots, feats, width), BF16),
            VMEM((slots // chunks * feats, width), F32),
            VMEM((feats, slots, width), BF16),
            VMEM((feats, rows, width), I32),
            VMEM((rows, feats * width), BF16),
            pltpu.SemaphoreType.DMA((chunks,)),
        ],
        compiler_params=params(48),
        cost_estimate=SMALL,
        name="pool",
    )(send_counts, spots, lengths, bag_items)


def order_kernel(group, rows, slots_ref, head_ref, out_ref):
    sources = slots_ref.shape[0]
    width = sources * CAP
    lane = lax.broadcasted_iota(I32, (1, width), 1).astype(F32)
    place = lax.broadcasted_iota(I32, (rows, width), 0).astype(F32)
    for g, a in enumerate(group):
        want = jnp.full((1, width), -1.0, F32)
        at = jnp.zeros((1, width), F32)
        for k in range(sources):
            count = head_ref[k, a : a + 1, :].astype(F32)
            count = jnp.concatenate([count] * (width // count.shape[1]), axis=1)
            slot = lane - k * CAP
            want = jnp.where((slot >= 0) & (slot < count), slot + at, want)
            at = at + count
        pick = jnp.where(want == place, 1.0, 0.0).astype(BF16)
        got = slots_ref[:, g * CAP : (g + 1) * CAP, :].reshape(width, slots_ref.shape[2])
        out_ref[g] = jnp.dot(pick, got, preferred_element_type=F32).astype(BF16)


def order(slots, head, group, rows):
    quarter = slots.shape[2]
    return pl.pallas_call(
        functools.partial(order_kernel, group, rows),
        out_shape=jax.ShapeDtypeStruct((len(group), rows, quarter), BF16),
        in_specs=[pl.BlockSpec(memory_space=VMEM), pl.BlockSpec(memory_space=VMEM)],
        out_specs=pl.BlockSpec(memory_space=VMEM),
        compiler_params=params(32),
        cost_estimate=SMALL,
        name="order",
    )(slots, head)


def cut_kernel(source_ref, out_ref):
    out_ref[...] = source_ref[...]


def cut(weight, low, high, tile):
    depth = weight.shape[1]
    return pl.pallas_call(
        cut_kernel,
        out_shape=jax.ShapeDtypeStruct((high - low, depth), BF16),
        grid=((high - low) // tile,),
        in_specs=[pl.BlockSpec((tile, depth), lambda n: (n + low // tile, 0))],
        out_specs=pl.BlockSpec((tile, depth), lambda n: (n, 0)),
        compiler_params=params(12),
        cost_estimate=SMALL,
        name="cut",
    )(weight)


def multiply_kernel(counts, spans, spot_ref, place_ref, *refs):
    groups, count = counts
    pieces = refs[: groups * count]
    own_ref = refs[groups * count]
    other_refs = refs[groups * count + 1 : groups * count + 1 + len(spans)]
    out_refs = refs[groups * count + 1 + len(spans) : -1]
    held = refs[-1]
    rows = out_refs[0].shape[0]
    step = pl.program_id(0)

    @pl.when(step == 0)
    def _():
        for g in range(groups):
            for j in range(count):
                piece = pieces[g * count + j]
                for k in range(piece.shape[0]):
                    which = g * piece.shape[0] + k
                    at = pl.multiple_of(place_ref[which] * rows, rows)
                    held[spot_ref[j], pl.ds(at, rows), :] = piece[k]

    quarter = held.shape[2]
    half = count // 2

    def run(other_ref):
        total = None
        for j in range(count):
            weight = own_ref if j < half else other_ref
            part = lax.dot_general(
                held[j],
                weight[:, (j % half) * quarter : (j % half + 1) * quarter],
                (((1,), (1,)), ((), ())),
                preferred_element_type=F32,
            )
            total = part if total is None else total + part
        for k, out_ref in enumerate(out_refs):
            out_ref[...] = total[k * rows : (k + 1) * rows].astype(BF16)

    for (low, high), other_ref in zip(spans, other_refs):
        pl.when((step >= low) & (step < high))(functools.partial(run, other_ref))


def multiply(spots, places, groups, own, others, offset, tile):
    blocks, rows, quarter = groups[0][0].shape
    count = len(groups[0])
    depth = own.shape[1]
    base = offset // tile
    total = blocks * len(groups)
    spans, at = [], 0
    for other in others:
        spans.append((at, at + other.shape[0] // tile))
        at = spans[-1][1]

    def other_spec(low, high):
        return pl.BlockSpec((tile, depth), lambda n: (jnp.clip(n - low, 0, high - low - 1), 0))

    return pl.pallas_call(
        functools.partial(multiply_kernel, (len(groups), count), spans),
        out_shape=[jax.ShapeDtypeStruct((rows, at * tile), BF16) for _ in range(total)],
        grid=(at,),
        in_specs=[pl.BlockSpec(memory_space=SMEM)] * 2
        + [
            pl.BlockSpec((blocks, rows, quarter), lambda n: (0, 0, 0), pipeline_mode=pl.Buffered(1))
            for _ in range(count * len(groups))
        ]
        + [pl.BlockSpec((tile, depth), lambda n: (n + base, 0))]
        + [other_spec(*span) for span in spans],
        out_specs=[pl.BlockSpec((rows, tile), lambda n: (0, n)) for _ in range(total)],
        scratch_shapes=[VMEM((count, total * rows, quarter), BF16)],
        compiler_params=params(40),
        cost_estimate=SMALL,
        name="multiply",
    )(spots, places, *[piece for group in groups for piece in group], own, *others)


def finish_kernel(end_ref, own_end, own_mid, outer, near, far, base_ref, bias_ref, *rest):
    out_ref = rest[-1]
    base = base_ref[0].astype(F32)
    is_end = end_ref[0] == 1

    def run(sums):
        product = sums[0][...].astype(F32)
        for extra in sums[1:]:
            product += extra[...].astype(F32)
        out_ref[...] = (base * (product + bias_ref[...]) + base).astype(BF16)

    pl.when(is_end)(functools.partial(run, (own_end, outer)))
    pl.when(jnp.logical_not(is_end))(functools.partial(run, (own_mid, near, far)))


def finish(is_end, sums, base, bias, offset, tile, onto=None):
    quarters, rows, quarter = base.shape
    first = offset // tile
    per = quarter // tile
    more = [] if onto is None else [onto]
    return pl.pallas_call(
        finish_kernel,
        out_shape=jax.ShapeDtypeStruct((rows, quarters * quarter), BF16),
        grid=(sums[0].shape[1] // tile,),
        in_specs=[pl.BlockSpec(memory_space=SMEM)]
        + [pl.BlockSpec((rows, tile), lambda n: (0, n))] * 5
        + [
            pl.BlockSpec((1, rows, tile), lambda n: ((n + first) // per, 0, (n + first) % per)),
            pl.BlockSpec((1, tile), lambda n: (0, n + first)),
        ]
        + [pl.BlockSpec(memory_space=ANY) for _ in more],
        out_specs=pl.BlockSpec((rows, tile), lambda n: (0, n + first)),
        input_output_aliases={8: 0} if more else {},
        compiler_params=params(12),
        cost_estimate=SMALL,
        name="finish",
    )(is_end, *sums, base, bias, *more)


def pick(index, options):
    value = options[0][1]
    for which, other in options[1:]:
        value = jnp.where(index == which, other, value)
    return value


def shards(bag_items, bag_lengths, send_counts, cross_weight, cross_bias):
    line, share = lax.axis_size("a"), lax.axis_size("b")
    tall = lax.axis_size("y")
    quarters = tall * 2
    rows = bag_lengths.shape[0]
    a, b = lax.axis_index("a"), lax.axis_index("b")
    y, c = lax.axis_index("y"), lax.axis_index("c")
    swap = [(0, 1), (1, 0)]
    edge = line // 4
    groups = [
        list(range(edge, line - edge)),
        list(range(edge)) + list(range(line - edge, line)),
    ]

    weight = cross_weight[0]
    outs = weight.shape[0]
    eighth = outs // 8
    tile = 2 * eighth
    parts = [(0, tile), (tile, 2 * tile), (2 * tile, outs)]

    def fetch(which, source):
        return lax.ppermute(cut(source, *parts[which], tile), "b", swap)

    quarter = bag_items.shape[1] * bag_items.shape[2] // quarters
    lengths = bag_lengths.T
    others = [fetch(0, weight), fetch(1, weight)]
    mixed = []
    if tall == 2:
        feats = bag_items.shape[1] // 2
        near = [(y ^ (k // 2)) * 2 + (c ^ (k % 2)) for k in range(4)]

        def half_pool(side):
            spots = jnp.stack([c, 1 - c, side]).astype(I32)
            part = lax.dynamic_slice_in_dim(lengths, side * feats, feats, 0)
            return list(pool(bag_items, part, send_counts, spots, groups, share, quarter))

        leaving = half_pool(1 - y)
        away = [lax.ppermute(piece, "y", swap) for piece in leaving]
        staying = half_pool(y)
        for g in range(2):
            staying[g], others[g] = lax.optimization_barrier((staying[g], others[g]))
            side = lax.ppermute(staying[g][1], "c", swap)
            cross = lax.ppermute(away[g][1], "c", swap)
            got = [staying[g][0], side, away[g][0], cross]
            mixed.append(
                jnp.stack([pick(near[q], [(k, got[k]) for k in range(4)]) for q in range(4)])
            )
    else:
        spots = jnp.arange(quarters, dtype=I32)
        for padded in pool(bag_items, lengths, send_counts, spots, groups, share, quarter):
            mixed.append(lax.all_to_all(padded, ("y", "c"), 0, 0, tiled=True))

    upper = a >= 2
    is_end = ((a == 0) | (a == 3)).astype(I32).reshape(1)
    flip = jnp.where(upper, 0, 1).astype(I32)
    places = jnp.stack([flip, 1 - flip])
    inward, middle, outward = [(0, 1), (3, 2)], [(1, 2), (2, 1)], [(1, 0), (2, 3)]

    ordered, pieces = [], []
    head = None
    for g, group in enumerate(groups):
        sent = mixed[g].reshape(line * share, mixed[g].shape[2], mixed[g].shape[3])
        slots = lax.all_to_all(sent, ("a", "b"), 0, 0, tiled=True)
        if head is None:
            head = slots[:, len(group) * CAP :, : bag_items.shape[2]]
        if g == 1 and line == 4:
            far1, near1 = multiply(spots, places, [pieces[0]], weight, others[:2], 0, tile)
            in2 = lax.ppermute(far1, "a", inward)
            in3 = lax.ppermute(near1, "a", inward)
            slots, far1 = lax.optimization_barrier((slots, far1))
        mine = order(slots, head, group, rows)
        if g == 0:
            late, mine = lax.optimization_barrier((weight, mine))
            others.append(fetch(2, late))
        ordered.append(mine)
        if tall == 2:
            far = lax.ppermute(mine, "y", swap)
            found = [(y, mine), (1 - y, far)]
        else:
            every = lax.all_gather(mine, "y", axis=0)
            found = [(jnp.int32(k), every[k]) for k in range(tall)]
        found = [(k, c, piece) for k, piece in found] + [
            (k, 1 - c, lax.ppermute(piece, "c", swap)) for k, piece in found
        ]
        pieces.append([piece for _, _, piece in found])
        spots = [k * 2 + core for k, core, _ in found]
        half = quarters // 2
        spots = jnp.stack([jnp.where(q // half == b, 0, half) + q % half for q in spots])
        spots = spots.astype(I32)

    blocks = [None] * line
    for g, group in enumerate(groups):
        for k, which in enumerate(group):
            blocks[which] = ordered[g][k]
    middle_piece = len(pieces[1]) // 2
    stacked, pieces[1][middle_piece] = lax.optimization_barrier(
        (jnp.stack(blocks), pieces[1][middle_piece])
    )
    back = lax.all_to_all(stacked, "a", 0, 0, tiled=True)

    if line != 4:
        where = jnp.arange(line, dtype=I32)
        columns = []
        for held, low in ((others[:2], 0), (others[2:], parts[2][0])):
            block = {}
            for g, group in enumerate(groups):
                partial = multiply(spots, where, [pieces[g]], weight, held, low, tile)
                block.update(zip(group, partial))
            up = down = None
            for s in range(1, line):
                send_up = pick(a, [(i, block[line - s + i]) for i in range(s)])
                send_down = pick(a, [(line - 1 - i, block[s - 1 - i]) for i in range(s)])
                if up is not None:
                    send_up = send_up + up
                    send_down = send_down + down
                up = lax.ppermute(send_up, "a", [(i, i + 1) for i in range(s)])
                down = lax.ppermute(
                    send_down, "a", [(line - 1 - i, line - 2 - i) for i in range(s)]
                )
            mine = pick(a, [(i, block[i]) for i in range(line)])
            columns.append(mine.astype(F32) + up.astype(F32) + down.astype(F32))
        back = lax.all_to_all(back, ("y", "c"), 0, 0, tiled=True)
        base = jnp.transpose(back, (1, 0, 2)).reshape(rows, -1).astype(F32)
        return (base * (jnp.concatenate(columns, axis=1) + cross_bias[0]) + base).astype(BF16)

    far0, near0 = multiply(spots, places, [pieces[1]], weight, others[:2], 0, tile)
    in1 = lax.ppermute(far0, "a", inward)
    both, far0 = lax.optimization_barrier((pieces, far0))
    mid3 = lax.ppermute(far1 + in2, "a", middle)
    mid2 = lax.ppermute(far0 + in1, "a", middle)
    out3 = lax.ppermute(near0 + mid2, "a", outward)
    sums = (near0, near1, out3, in3, mid3)
    back = lax.all_to_all(back, ("y", "c"), 0, 0, tiled=True)

    far1, near1, far0, near0 = multiply(
        spots, jnp.concatenate([places, places + 2]), both, weight, others[2:], parts[2][0], tile
    )
    result = finish(is_end, sums, back, cross_bias, 0, tile)
    in1 = lax.ppermute(far0, "a", inward)
    in2 = lax.ppermute(far1, "a", inward)
    mid2 = lax.ppermute(far0 + in1, "a", middle)
    in3 = lax.ppermute(near1, "a", inward)
    mid3 = lax.ppermute(far1 + in2, "a", middle)
    out3 = lax.ppermute(near0 + mid2, "a", outward)
    sums = (near0, near1, out3, in3, mid3)
    return finish(is_end, sums, back, cross_bias, parts[2][0], tile, result)


def solution(mesh):
    owners, tensor = mesh.devices.shape
    split = Mesh(
        mesh.devices.reshape(tensor, owners // tensor, tensor // 2, 2), ("a", "b", "y", "c")
    )
    dp, tp = ("a", "b"), ("y", "c")
    return jax.shard_map(
        shards,
        mesh=split,
        in_specs=(
            P(dp, tp, None),
            P(dp, tp),
            P(dp, None),
            P(None, tp, dp),
            P(None, tp),
        ),
        out_specs=P(dp, tp),
        check_vma=False,
    )
```

```python
import functools

import jax
import jax.numpy as jnp
from jax import lax
from jax.experimental import pallas as pl
from jax.experimental.pallas import tpu as pltpu
from jax.sharding import Mesh
from jax.sharding import PartitionSpec as P

CAP = 48
HEAD = 16
BF16 = jnp.bfloat16
F32 = jnp.float32
I32 = jnp.int32
ANY = pl.ANY
VMEM = pltpu.VMEM
SMEM = pltpu.SMEM
SMALL = pl.CostEstimate(flops=1, bytes_accessed=1, transcendentals=0)


def params(mib):
    return pltpu.CompilerParams(vmem_limit_bytes=mib << 20)


def pool_kernel(groups, share, quarter, whole, count_ref, spot_ref, length_ref, items_ref, *rest):
    out_refs = rest[: len(groups)]
    items, wide, by_feat, last, pooled, sems = rest[len(groups) :]
    slots, feats, width = items.shape
    rows = length_ref.shape[1]
    step = slots // sems.shape[0]
    copies = []
    for k in range(sems.shape[0]):
        part = pl.ds(k * step, step)
        if whole:
            source = items_ref.at[part]
        else:
            start = pl.multiple_of(spot_ref[spot_ref.shape[0] - 1] * feats, feats)
            source = items_ref.at[part, pl.ds(start, feats)]
        copy = pltpu.make_async_copy(source, items.at[part], sems.at[k])
        copy.start()
        copies.append(copy)

    row_id = lax.broadcasted_iota(I32, (rows, rows), 0)
    col_id = lax.broadcasted_iota(I32, (rows, rows), 1)
    lower = jnp.where(col_id <= row_id, 1.0, 0.0).astype(BF16)
    lengths = length_ref[...].astype(F32).astype(BF16)
    dims = (((1,), (1,)), ((), ()))
    ends = lax.dot_general(lower, lengths, dims, preferred_element_type=F32).astype(I32)
    for f in range(feats):
        last[f] = jnp.broadcast_to(ends[:, f : f + 1], (rows, width))

    for k in range(sems.shape[0]):
        copies[k].wait()
        part = pl.ds(k * step, step)
        wide[: step * feats] = items[part].astype(F32).reshape(step * feats, width)
        for f in range(feats):
            by_feat[f, part, :] = wide[pl.ds(f, step, stride=feats), :].astype(BF16)

    lane = lax.broadcasted_iota(I32, (1, width), 1)
    top = lax.broadcasted_iota(I32, (rows, width), 0) == 0

    @pl.loop(0, feats, unroll=2)
    def _(f):
        high = last[f]
        tiles = []
        for k in range(slots // width):
            tiles.append(jnp.where(lane + k * width < high, 1.0, 0.0).astype(BF16))
        total = jnp.dot(jnp.concatenate(tiles, axis=1), by_feat[f], preferred_element_type=F32)
        above = jnp.where(top, 0.0, pltpu.roll(total, 1, 0))
        pooled[:, pl.ds(pl.multiple_of(f * width, width), width)] = (total - above).astype(BF16)

    slot = lax.broadcasted_iota(I32, (CAP, rows), 0)
    source = lax.broadcasted_iota(I32, (CAP, rows), 1)
    begin = []
    at = jnp.int32(0)
    for p in range(count_ref.shape[1]):
        begin.append(at)
        at = at + count_ref[0, p]
    for g, group in enumerate(groups):
        picks = []
        for b in range(share):
            for a in group:
                p = a * share + b
                hit = (source == slot + begin[p]) & (slot < count_ref[0, p])
                picks.append(jnp.where(hit, 1.0, 0.0).astype(BF16))
        pick = jnp.concatenate(picks, axis=0)
        body = len(group) * CAP
        for q in range(out_refs[g].shape[0]):
            at = pl.multiple_of(spot_ref[q] * quarter, quarter)
            moved = jnp.dot(
                pick, pooled[:, pl.ds(at, quarter)], preferred_element_type=F32
            ).astype(BF16)
            for b in range(share):
                out_refs[g][q, b, :body] = moved[b * body : (b + 1) * body]
        if g > 0:
            continue
        which = lax.broadcasted_iota(I32, (HEAD, quarter), 0)
        for b in range(share):
            head = jnp.zeros((HEAD, quarter), F32)
            for p in range(b, count_ref.shape[1], share):
                head = jnp.where(which == p // share, count_ref[0, p].astype(F32), head)
            for q in range(out_refs[g].shape[0]):
                out_refs[g][q, b, body:] = head.astype(BF16)


def pool(bag_items, lengths, send_counts, spots, groups, share, quarter):
    slots, whole, width = bag_items.shape
    feats, rows = lengths.shape
    quarters = feats * width // quarter
    chunks = 8
    return pl.pallas_call(
        functools.partial(pool_kernel, groups, share, quarter, feats == whole),
        out_shape=[
            jax.ShapeDtypeStruct(
                (quarters, share, len(g) * CAP + (0 if k else HEAD), quarter), BF16
            )
            for k, g in enumerate(groups)
        ],
        in_specs=[
            pl.BlockSpec(memory_space=SMEM),
            pl.BlockSpec(memory_space=SMEM),
            pl.BlockSpec(memory_space=VMEM),
            pl.BlockSpec(memory_space=ANY),
        ],
        out_specs=[pl.BlockSpec(memory_space=VMEM) for _ in groups],
        scratch_shapes=[
            VMEM((slots, feats, width), BF16),
            VMEM(((slots // chunks + 1) * feats, width), F32),
            VMEM((feats, slots, width), BF16),
            VMEM((feats, rows, width), I32),
            VMEM((rows, feats * width), BF16),
            pltpu.SemaphoreType.DMA((chunks,)),
        ],
        compiler_params=params(48),
        cost_estimate=SMALL,
        name="pool",
    )(send_counts, spots, lengths, bag_items)


def order_kernel(group, rows, slots_ref, head_ref, out_ref):
    sources = slots_ref.shape[0]
    width = sources * CAP
    lane = lax.broadcasted_iota(I32, (1, width), 1).astype(F32)
    place = lax.broadcasted_iota(I32, (rows, width), 0).astype(F32)
    for g, a in enumerate(group):
        want = jnp.full((1, width), -1.0, F32)
        at = jnp.zeros((1, width), F32)
        for k in range(sources):
            count = head_ref[k, a : a + 1, :].astype(F32)
            count = jnp.concatenate([count] * (width // count.shape[1]), axis=1)
            slot = lane - k * CAP
            want = jnp.where((slot >= 0) & (slot < count), slot + at, want)
            at = at + count
        pick = jnp.where(want == place, 1.0, 0.0).astype(BF16)
        got = slots_ref[:, g * CAP : (g + 1) * CAP, :].reshape(width, slots_ref.shape[2])
        out_ref[g] = jnp.dot(pick, got, preferred_element_type=F32).astype(BF16)


def order(slots, head, group, rows):
    quarter = slots.shape[2]
    return pl.pallas_call(
        functools.partial(order_kernel, group, rows),
        out_shape=jax.ShapeDtypeStruct((len(group), rows, quarter), BF16),
        in_specs=[pl.BlockSpec(memory_space=VMEM), pl.BlockSpec(memory_space=VMEM)],
        out_specs=pl.BlockSpec(memory_space=VMEM),
        compiler_params=params(32),
        cost_estimate=SMALL,
        name="order",
    )(slots, head)


def cut_kernel(source_ref, out_ref):
    out_ref[...] = source_ref[...]


def cut(weight, low, high, tile):
    depth = weight.shape[1]
    return pl.pallas_call(
        cut_kernel,
        out_shape=jax.ShapeDtypeStruct((high - low, depth), BF16),
        grid=((high - low) // tile,),
        in_specs=[pl.BlockSpec((tile, depth), lambda n: (n + low // tile, 0))],
        out_specs=pl.BlockSpec((tile, depth), lambda n: (n, 0)),
        compiler_params=params(12),
        cost_estimate=SMALL,
        name="cut",
    )(weight)


def multiply_kernel(counts, spans, spot_ref, place_ref, *refs):
    groups, count = counts
    pieces = refs[: groups * count]
    own_ref = refs[groups * count]
    other_refs = refs[groups * count + 1 : groups * count + 1 + len(spans)]
    out_refs = refs[groups * count + 1 + len(spans) : -1]
    held = refs[-1]
    rows = out_refs[0].shape[0]
    step = pl.program_id(0)

    @pl.when(step == 0)
    def _():
        for g in range(groups):
            for j in range(count):
                piece = pieces[g * count + j]
                for k in range(piece.shape[0]):
                    which = g * piece.shape[0] + k
                    at = pl.multiple_of(place_ref[which] * rows, rows)
                    held[spot_ref[j], pl.ds(at, rows), :] = piece[k]

    quarter = held.shape[2]
    half = count // 2

    def run(other_ref):
        total = None
        for j in range(count):
            weight = own_ref if j < half else other_ref
            part = lax.dot_general(
                held[j],
                weight[:, (j % half) * quarter : (j % half + 1) * quarter],
                (((1,), (1,)), ((), ())),
                preferred_element_type=F32,
            )
            total = part if total is None else total + part
        for k, out_ref in enumerate(out_refs):
            out_ref[...] = total[k * rows : (k + 1) * rows].astype(BF16)

    for (low, high), other_ref in zip(spans, other_refs):
        pl.when((step >= low) & (step < high))(functools.partial(run, other_ref))


def multiply(spots, places, groups, own, others, offset, tile):
    blocks, rows, quarter = groups[0][0].shape
    count = len(groups[0])
    depth = own.shape[1]
    base = offset // tile
    total = blocks * len(groups)
    spans, at = [], 0
    for other in others:
        spans.append((at, at + other.shape[0] // tile))
        at = spans[-1][1]

    def other_spec(low, high):
        return pl.BlockSpec((tile, depth), lambda n: (jnp.clip(n - low, 0, high - low - 1), 0))

    return pl.pallas_call(
        functools.partial(multiply_kernel, (len(groups), count), spans),
        out_shape=[jax.ShapeDtypeStruct((rows, at * tile), BF16) for _ in range(total)],
        grid=(at,),
        in_specs=[pl.BlockSpec(memory_space=SMEM)] * 2
        + [
            pl.BlockSpec((blocks, rows, quarter), lambda n: (0, 0, 0), pipeline_mode=pl.Buffered(1))
            for _ in range(count * len(groups))
        ]
        + [pl.BlockSpec((tile, depth), lambda n: (n + base, 0))]
        + [other_spec(*span) for span in spans],
        out_specs=[pl.BlockSpec((rows, tile), lambda n: (0, n)) for _ in range(total)],
        scratch_shapes=[VMEM((count, total * rows, quarter), BF16)],
        compiler_params=params(40),
        cost_estimate=SMALL,
        name="multiply",
    )(spots, places, *[piece for group in groups for piece in group], own, *others)


def finish_kernel(end_ref, own_end, own_mid, outer, near, far, base_ref, bias_ref, *rest):
    out_ref = rest[-1]
    base = base_ref[0].astype(F32)
    is_end = end_ref[0] == 1

    def run(sums):
        product = sums[0][...].astype(F32)
        for extra in sums[1:]:
            product += extra[...].astype(F32)
        out_ref[...] = (base * (product + bias_ref[...]) + base).astype(BF16)

    pl.when(is_end)(functools.partial(run, (own_end, outer)))
    pl.when(jnp.logical_not(is_end))(functools.partial(run, (own_mid, near, far)))


def finish(is_end, sums, base, bias, offset, tile, onto=None):
    quarters, rows, quarter = base.shape
    first = offset // tile
    per = quarter // tile
    more = [] if onto is None else [onto]
    return pl.pallas_call(
        finish_kernel,
        out_shape=jax.ShapeDtypeStruct((rows, quarters * quarter), BF16),
        grid=(sums[0].shape[1] // tile,),
        in_specs=[pl.BlockSpec(memory_space=SMEM)]
        + [pl.BlockSpec((rows, tile), lambda n: (0, n))] * 5
        + [
            pl.BlockSpec((1, rows, tile), lambda n: ((n + first) // per, 0, (n + first) % per)),
            pl.BlockSpec((1, tile), lambda n: (0, n + first)),
        ]
        + [pl.BlockSpec(memory_space=ANY) for _ in more],
        out_specs=pl.BlockSpec((rows, tile), lambda n: (0, n + first)),
        input_output_aliases={8: 0} if more else {},
        compiler_params=params(12),
        cost_estimate=SMALL,
        name="finish",
    )(is_end, *sums, base, bias, *more)


def pick(index, options):
    value = options[0][1]
    for which, other in options[1:]:
        value = jnp.where(index == which, other, value)
    return value


def shards(bag_items, bag_lengths, send_counts, cross_weight, cross_bias):
    line, share = lax.axis_size("a"), lax.axis_size("b")
    tall = lax.axis_size("y")
    quarters = tall * 2
    rows = bag_lengths.shape[0]
    a, b = lax.axis_index("a"), lax.axis_index("b")
    y, c = lax.axis_index("y"), lax.axis_index("c")
    swap = [(0, 1), (1, 0)]
    edge = line // 4
    groups = [
        list(range(edge, line - edge)),
        list(range(edge)) + list(range(line - edge, line)),
    ]

    weight = cross_weight[0]
    outs = weight.shape[0]
    eighth = outs // 8
    tile = 2 * eighth
    parts = [(0, tile), (tile, 2 * tile), (2 * tile, outs)]

    def fetch(which, source):
        return lax.ppermute(cut(source, *parts[which], tile), "b", swap)

    quarter = bag_items.shape[1] * bag_items.shape[2] // quarters
    lengths = bag_lengths.T
    others = [fetch(0, weight), fetch(1, weight)]
    mixed = []
    if tall == 2:
        feats = bag_items.shape[1] // 2
        near = [(y ^ (k // 2)) * 2 + (c ^ (k % 2)) for k in range(4)]

        def half_pool(side):
            spots = jnp.stack([c, 1 - c, side]).astype(I32)
            part = lax.dynamic_slice_in_dim(lengths, side * feats, feats, 0)
            return list(pool(bag_items, part, send_counts, spots, groups, share, quarter))

        leaving = half_pool(1 - y)
        away = [lax.ppermute(piece, "y", swap) for piece in leaving]
        staying = half_pool(y)
        for g in range(2):
            staying[g], others[g] = lax.optimization_barrier((staying[g], others[g]))
            side = lax.ppermute(staying[g][1], "c", swap)
            cross = lax.ppermute(away[g][1], "c", swap)
            got = [staying[g][0], side, away[g][0], cross]
            mixed.append(
                jnp.stack([pick(near[q], [(k, got[k]) for k in range(4)]) for q in range(4)])
            )
    else:
        spots = jnp.arange(quarters, dtype=I32)
        for padded in pool(bag_items, lengths, send_counts, spots, groups, share, quarter):
            mixed.append(lax.all_to_all(padded, ("y", "c"), 0, 0, tiled=True))

    upper = a >= 2
    is_end = ((a == 0) | (a == 3)).astype(I32).reshape(1)
    flip = jnp.where(upper, 0, 1).astype(I32)
    places = jnp.stack([flip, 1 - flip])
    inward, middle, outward = [(0, 1), (3, 2)], [(1, 2), (2, 1)], [(1, 0), (2, 3)]

    ordered, pieces = [], []
    head = None
    for g, group in enumerate(groups):
        sent = mixed[g].reshape(line * share, mixed[g].shape[2], mixed[g].shape[3])
        slots = lax.all_to_all(sent, ("a", "b"), 0, 0, tiled=True)
        if head is None:
            head = slots[:, len(group) * CAP :, : bag_items.shape[2]]
        if g == 1 and line == 4:
            far1, near1 = multiply(spots, places, [pieces[0]], weight, others[:2], 0, tile)
            in2 = lax.ppermute(far1, "a", inward)
            in3 = lax.ppermute(near1, "a", inward)
            slots, far1 = lax.optimization_barrier((slots, far1))
        mine = order(slots, head, group, rows)
        if g == 0:
            late, mine = lax.optimization_barrier((weight, mine))
            others.append(fetch(2, late))
        ordered.append(mine)
        if tall == 2:
            far = lax.ppermute(mine, "y", swap)
            found = [(y, mine), (1 - y, far)]
        else:
            every = lax.all_gather(mine, "y", axis=0)
            found = [(jnp.int32(k), every[k]) for k in range(tall)]
        found = [(k, c, piece) for k, piece in found] + [
            (k, 1 - c, lax.ppermute(piece, "c", swap)) for k, piece in found
        ]
        pieces.append([piece for _, _, piece in found])
        spots = [k * 2 + core for k, core, _ in found]
        half = quarters // 2
        spots = jnp.stack([jnp.where(q // half == b, 0, half) + q % half for q in spots])
        spots = spots.astype(I32)

    blocks = [None] * line
    for g, group in enumerate(groups):
        for k, which in enumerate(group):
            blocks[which] = ordered[g][k]
    middle_piece = len(pieces[1]) // 2
    stacked, pieces[1][middle_piece] = lax.optimization_barrier(
        (jnp.stack(blocks), pieces[1][middle_piece])
    )
    back = lax.all_to_all(stacked, "a", 0, 0, tiled=True)

    if line != 4:
        where = jnp.arange(line, dtype=I32)
        columns = []
        for held, low in ((others[:2], 0), (others[2:], parts[2][0])):
            block = {}
            for g, group in enumerate(groups):
                partial = multiply(spots, where, [pieces[g]], weight, held, low, tile)
                block.update(zip(group, partial))
            up = down = None
            for s in range(1, line):
                send_up = pick(a, [(i, block[line - s + i]) for i in range(s)])
                send_down = pick(a, [(line - 1 - i, block[s - 1 - i]) for i in range(s)])
                if up is not None:
                    send_up = send_up + up
                    send_down = send_down + down
                up = lax.ppermute(send_up, "a", [(i, i + 1) for i in range(s)])
                down = lax.ppermute(
                    send_down, "a", [(line - 1 - i, line - 2 - i) for i in range(s)]
                )
            mine = pick(a, [(i, block[i]) for i in range(line)])
            columns.append(mine.astype(F32) + up.astype(F32) + down.astype(F32))
        back = lax.all_to_all(back, ("y", "c"), 0, 0, tiled=True)
        base = jnp.transpose(back, (1, 0, 2)).reshape(rows, -1).astype(F32)
        return (base * (jnp.concatenate(columns, axis=1) + cross_bias[0]) + base).astype(BF16)

    far0, near0 = multiply(spots, places, [pieces[1]], weight, others[:2], 0, tile)
    in1 = lax.ppermute(far0, "a", inward)
    both, far0 = lax.optimization_barrier((pieces, far0))
    mid3 = lax.ppermute(far1 + in2, "a", middle)
    mid2 = lax.ppermute(far0 + in1, "a", middle)
    out3 = lax.ppermute(near0 + mid2, "a", outward)
    sums = (near0, near1, out3, in3, mid3)
    back = lax.all_to_all(back, ("y", "c"), 0, 0, tiled=True)

    far1, near1, far0, near0 = multiply(
        spots, jnp.concatenate([places, places + 2]), both, weight, others[2:], parts[2][0], tile
    )
    result = finish(is_end, sums, back, cross_bias, 0, tile)
    in1 = lax.ppermute(far0, "a", inward)
    in2 = lax.ppermute(far1, "a", inward)
    mid2 = lax.ppermute(far0 + in1, "a", middle)
    in3 = lax.ppermute(near1, "a", inward)
    mid3 = lax.ppermute(far1 + in2, "a", middle)
    out3 = lax.ppermute(near0 + mid2, "a", outward)
    sums = (near0, near1, out3, in3, mid3)
    return finish(is_end, sums, back, cross_bias, parts[2][0], tile, result)


def solution(mesh):
    owners, tensor = mesh.devices.shape
    split = Mesh(
        mesh.devices.reshape(tensor, owners // tensor, tensor // 2, 2), ("a", "b", "y", "c")
    )
    dp, tp = ("a", "b"), ("y", "c")
    return jax.shard_map(
        shards,
        mesh=split,
        in_specs=(
            P(dp, tp, None),
            P(dp, tp),
            P(dp, None),
            P(None, tp, dp),
            P(None, tp),
        ),
        out_specs=P(dp, tp),
        check_vma=False,
    )
```
